256 devices in a mesh: region: 32 (over x, y, core), industry: 8 (over z).
Axes of the slice: x: 4, y: 4, z: 8, core: 2. Of those that a mesh axis runs over, the one named last changes fastest.
Arguments:
- position: bfloat16 [8, 1536, 16, 1024], P(None, 'region', None, 'industry'), may hold values from 0.049804688 to 0.94921875
- dual_lower: bfloat16 [8, 1536, 16, 1024], P(None, 'region', None, 'industry'), may hold values from 0.099609375 to 10
- dual_upper: bfloat16 [8, 1536, 16, 1024], P(None, 'region', None, 'industry'), may hold values from 0.099609375 to 10
- upper_bound: int32 [1536, 16, 1024], P('region', None, 'industry'), may hold values from 2 to 63
- suppressed: int32 [1536, 16, 1024], P('region', None, 'industry'), may hold values from 0 to 1
- attack_region: int32 [8], replicated, may hold values from 0 to 1535
- attack_column: int32 [8], replicated, may hold values from 0 to 16383
- dual_row: float32 [8, 1536, 16], P(None, 'region'), may hold values from -3 to 3
- dual_col: float32 [8, 16, 1024], P(None, None, 'industry'), may hold values from -3 to 3
Outputs:
- cell_step: bfloat16 [8, 1536, 16, 1024], P(None, 'region', None, 'industry')
- row_step: float32 [8, 1536, 16], P(None, 'region')
- col_step: float32 [8, 16, 1024], P(None, None, 'industry')
The draws below stay inside these ranges and needn't reach their ends.
All inputs are finite; a program needn't handle non-finite values.
Results may differ from the reference program's by a relative error of at most 0.001.
Values sent between devices are 32-bit elements; how exact they have to be, the bound alone decides.
A program may use at most 64 MiB of HBM per device.

```python
import math
import jax
import jax.numpy as jnp
from jax import lax

R = 1536
I = 1024
S = 16
K = 8
ITERS = 3


def shuffle_four(sub_key):
    return jax.random.permutation(sub_key, 4)


def block_plan(key):
    plan_key = jax.random.fold_in(key, 40961)
    region_keys = jax.random.split(jax.random.fold_in(plan_key, 1), S)
    industry_keys = jax.random.split(jax.random.fold_in(plan_key, 2), S)
    region_order = jax.vmap(shuffle_four)(region_keys).astype(jnp.int32)
    industry_order = jax.vmap(shuffle_four)(industry_keys).astype(jnp.int32)
    strong_level = jax.random.randint(jax.random.fold_in(plan_key, 3), (S,), 6, 9)
    return (region_order, industry_order, strong_level)


def quarter_signs(block_order, cell_count):
    quarter = jnp.arange(cell_count, dtype=jnp.int32) * 4 // cell_count
    place_rank = block_order[:, quarter].T
    first_sign = 1 - 2 * (place_rank // 2)
    second_sign = 1 - 2 * (place_rank % 2)
    return (first_sign, second_sign)


def draw_suppressed(key, part):
    region_order, industry_order, strong_level = block_plan(key)
    reg_first, reg_second = quarter_signs(region_order, R)
    ind_first, ind_second = quarter_signs(industry_order, I)
    weak_level = 9 - strong_level
    density_level = 10 + strong_level[None, :, None] * reg_first[:, :, None] * ind_first.T[None] + weak_level[None, :, None] * reg_second[:, :, None] * ind_second.T[None]
    ticket = jax.random.randint(jax.random.fold_in(key, 40962), (R, S, I), 0, 20)
    return (ticket < density_level).astype(jnp.int32)


def draw_dual_row(key, part):
    region_order, industry_order, strong_level = block_plan(key)
    reg_first, reg_second = quarter_signs(region_order, R)
    noise_key = jax.random.fold_in(key, 40963)
    first_part = reg_first.astype(jnp.float32)
    second_part = reg_second.astype(jnp.float32)
    noise_part = jnp.clip(0.4 * jax.random.normal(noise_key, (K, R, S), jnp.float32), -1.6, 1.6)
    mean_part = 0.9 * first_part + 0.3 * second_part
    return (mean_part[None] + noise_part).astype(jnp.float32)


def place_ends(drawn, rng, smallest, largest):
    longest = drawn.shape.index(max(drawn.shape))
    spots = []
    for shift in (0, 1):
        where = [jax.random.randint(jax.random.fold_in(rng, axis), (), 0, length) for axis, length in enumerate(drawn.shape)]
        where[longest] = (where[longest] + shift) % drawn.shape[longest]
        spots.append(tuple(where))
    return drawn.at[spots[0]].set(smallest).at[spots[1]].set(largest)


def shard_levels(own_key, dims, cuts, smallest, top_value):
    level, own = 1.0, jax.random.fold_in(own_key, 6)
    for dim, shards_of in cuts:
        steps = jnp.exp(jax.random.uniform(jax.random.fold_in(own, dim), (shards_of,), jnp.float32, smallest / len(cuts), top_value / len(cuts)))
        level = level * jnp.repeat(steps, dims[dim] // shards_of).reshape([-1 if axis == dim else 1 for axis in range(len(dims))])
    return level


def gaussian(key, extent, width, most, pieces=(), kind=jnp.bfloat16):
    result = width * jax.random.normal(key, extent, jnp.float32)
    if pieces:
        result = result * shard_levels(key, extent, pieces, -0.22, 0.18)
    return jnp.clip(result, -most, most).astype(kind)


def setup_inputs(seed: int = 0) -> dict:
    key_list = jax.random.split(jax.random.key(seed), 10)
    position = jnp.clip(0.049804688 + 0.89941406 * jax.random.uniform(key_list[0], (K, R, S, I), jnp.float32) ** shard_levels(key_list[0], (K, R, S, I), ((1, 32), (3, 8)), -0.2, 0.2), 0.049804688, 0.94921875).astype(jnp.bfloat16)
    dual_lower = jnp.clip(jnp.exp(math.log(10.0) - 4.609084 * jax.random.uniform(key_list[1], (K, R, S, I), jnp.float32) ** shard_levels(key_list[1], (K, R, S, I), ((1, 32), (3, 8)), -0.2, 0.2)), 0.099609375, 10.0).astype(jnp.bfloat16)
    dual_upper = jnp.clip(jnp.exp(math.log(10.0) - 4.609084 * jax.random.uniform(key_list[2], (K, R, S, I), jnp.float32) ** shard_levels(key_list[2], (K, R, S, I), ((1, 32), (3, 8)), -0.2, 0.2)), 0.099609375, 10.0).astype(jnp.bfloat16)
    upper_bound = place_ends(jax.random.randint(key_list[3], (R, S, I), 2, 64), jax.random.fold_in(key_list[3], 1), 2, 63).astype(jnp.int32)
    suppressed = draw_suppressed(jax.random.fold_in(key_list[9], 71), 0)
    attack_region = place_ends(jax.random.randint(key_list[5], (K,), 0, R), jax.random.fold_in(key_list[5], 1), 0, R - 1).astype(jnp.int32)
    attack_column = place_ends(jax.random.randint(key_list[6], (K,), 0, S * I), jax.random.fold_in(key_list[6], 1), 0, (S * I) - 1).astype(jnp.int32)
    dual_row = draw_dual_row(jax.random.fold_in(key_list[9], 71), 0)
    dual_col = gaussian(key_list[8], (K, S, I), 0.5, 3.0, ((2, 8),), jnp.float32)
    return {"position": position, "dual_lower": dual_lower, "dual_upper": dual_upper, "upper_bound": upper_bound, "suppressed": suppressed, "attack_region": attack_region, "attack_column": attack_column, "dual_row": dual_row, "dual_col": dual_col}


weight_attack = 8.0
barrier = 0.5
shift_diag = 1.0


def inner_pair(first_row, second_row, first_col, second_col):
    return jnp.sum(first_row * second_row) + jnp.sum(first_col * second_col)


def reference(position, dual_lower, dual_upper, upper_bound, suppressed, attack_region, attack_column, dual_row, dual_col):
    upper = upper_bound.astype(jnp.float32)
    region_ids = jnp.arange(R, dtype=jnp.int32)
    column_ids = jnp.arange(S, dtype=jnp.int32)[:, None] * I + jnp.arange(I, dtype=jnp.int32)[None, :]

    def solve_one(items):
        pos_one, low_one, high_one, region_one, column_one, row_one, col_one = items
        attacked = (region_ids[:, None, None] == region_one) & (column_ids[None] == column_one)
        active = jnp.maximum(suppressed, attacked.astype(jnp.int32)).astype(jnp.float32)
        value = pos_one.astype(jnp.float32) * upper
        slack = upper - value
        scaling = active / (low_one.astype(jnp.float32) / value + high_one.astype(jnp.float32) / slack)
        gradient = jnp.where(attacked, jnp.float32(weight_attack), jnp.float32(0.0)) - row_one[:, :, None] - col_one[None] + barrier * (1.0 / value - 1.0 / slack)
        margin_term = active * (0.5 * upper - value) + scaling * gradient
        res_row = jnp.sum(margin_term, axis=2)
        res_col = jnp.sum(margin_term, axis=0)
        diag_row = jnp.sum(scaling, axis=2) + shift_diag
        diag_col = jnp.sum(scaling, axis=0) + shift_diag

        def couple(part_row, part_col):
            return jnp.sum(scaling * part_col[None], axis=2), jnp.sum(scaling * part_row[:, :, None], axis=0)

        def precondition(vec_row, vec_col):
            base_row, base_col = vec_row / diag_row, vec_col / diag_col
            once_row, once_col = couple(base_row, base_col)
            once_row, once_col = once_row / diag_row, once_col / diag_col
            twice_row, twice_col = couple(once_row, once_col)
            twice_row, twice_col = twice_row / diag_row, twice_col / diag_col
            return base_row - once_row + twice_row, base_col - once_col + twice_col

        pre_row, pre_col = precondition(res_row, res_col)
        dir_row, dir_col = pre_row, pre_col
        rz_now = inner_pair(res_row, pre_row, res_col, pre_col)
        sol_row = jnp.zeros_like(res_row)
        sol_col = jnp.zeros_like(res_col)
        for iteration in range(ITERS):
            image_row, image_col = couple(dir_row, dir_col)
            image_row = diag_row * dir_row + image_row
            image_col = diag_col * dir_col + image_col
            step_len = rz_now / inner_pair(dir_row, image_row, dir_col, image_col)
            sol_row = sol_row + step_len * dir_row
            sol_col = sol_col + step_len * dir_col
            res_row = res_row - step_len * image_row
            res_col = res_col - step_len * image_col
            if iteration + 1 < ITERS:
                pre_row, pre_col = precondition(res_row, res_col)
                rz_next = inner_pair(res_row, pre_row, res_col, pre_col)
                step_ratio = rz_next / rz_now
                dir_row = pre_row + step_ratio * dir_row
                dir_col = pre_col + step_ratio * dir_col
                rz_now = rz_next
        cell_step = (scaling * (sol_row[:, :, None] + sol_col[None] - gradient)).astype(jnp.bfloat16)
        return cell_step, sol_row, sol_col

    return lax.map(solve_one, (position, dual_lower, dual_upper, attack_region, attack_column, dual_row, dual_col))
```

```python
import jax
import jax.numpy as jnp
from jax import lax
from jax.experimental import pallas as pl
from jax.experimental.pallas import tpu as pltpu
from jax.sharding import PartitionSpec as P

MESH = pl.DeviceIdType.MESH
F32 = jnp.float32
BF16 = jnp.bfloat16
K, RL, S, IL = 8, 48, 16, 128
KO = 4
NZ, NX, NY = 8, 4, 4
ROUNDS = 8
WEIGHT_ATTACK, BARRIER, SHIFT = 8.0, 0.5, 1.0
Z_STEPS = (4, 3, 5, 2, 6, 1, 7)
LINE_STEPS = (2, 1, 3)


def split_pair(x):
    high = x.astype(BF16)
    low = (x - high.astype(F32)).astype(BF16)
    return high, low


def split_three(x):
    high = x.astype(BF16)
    rest = x - high.astype(F32)
    mid = rest.astype(BF16)
    low = (rest - mid.astype(F32)).astype(BF16)
    return jnp.concatenate([high, mid, low], axis=0)


def pack(rows):
    tiles = [rows[q][8 * h : 8 * h + 8] for q in range(KO) for h in range(2)]
    lane = lax.broadcasted_iota(jnp.int32, (8, 128), 1)
    packed = []
    for i in range(6):
        spare = pltpu.roll(tiles[6 + i // 3], 96 - 32 * (i % 3), 1)
        packed.append(jnp.where(lane < 96, tiles[i], spare))
    return jnp.concatenate(packed, axis=0)


def unpack(packed):
    lane = lax.broadcasted_iota(jnp.int32, (8, 128), 1)
    zero = jnp.zeros((8, 128), F32)
    m = [packed[8 * i : 8 * i + 8] for i in range(6)]
    tiles = [jnp.where(lane < 96, x, zero) for x in m]
    for g in range(2):
        a = pltpu.roll(m[3 * g], 32, 1)
        b = pltpu.roll(m[3 * g + 1], 64, 1)
        c = pltpu.roll(m[3 * g + 2], 96, 1)
        tiles.append(
            jnp.where(lane < 32, a, jnp.where(lane < 64, b, jnp.where(lane < 96, c, zero)))
        )
    return [jnp.concatenate([tiles[2 * q], tiles[2 * q + 1]], axis=0) for q in range(KO)]


def kernel(
    pos_hbm, low_hbm, high_hbm, upper_hbm, supp_hbm, att_r, att_c, drow_hbm, dcol_hbm,
    cell_hbm, row_out, col_out,
    pos, low, high, upper, supp, drow, dcol, in_sem, small_sem,
    scal, scal_x, grad, drow_b, umat, amat, hmat, key, part, part_x, pair_s, pair_r,
    mat_c, mat_r,
    ini_zs, ini_zr, ini_c1, ini_c1r, ini_c2, ini_c2r, ini_s, ini_r,
    zs, zr, z_ss, z_rs,
    c1, c1r, c2, c2r, c_ss, c_rs,
    dzs, dzr, dps, dpr, d_ss, d_rs,
    hist_r, hist_c, dia_r, dia_c, inv_r, inv_c, vec_r, vec_c, cur_r, cur_c, scl,
    fin, fin_x, fin_r, cell, out_sem,
):
    reg = lax.axis_index("region")
    iz = lax.axis_index("industry")
    core = lax.rem(reg, 2)
    iy = lax.rem(reg // 2, NY)
    ix = reg // (2 * NY)
    kb = core * KO
    ks = KO - kb
    sibling = {"region": reg + 1 - 2 * core}

    def plane(x, y):
        return {"region": (x * NY + y) * 2 + core}

    x_peers = [plane(lax.rem(ix + h, NX), iy) for h in LINE_STEPS]
    y_peers = [plane(ix, lax.rem(iy + h, NY)) for h in LINE_STEPS]
    z_peers = [{"industry": lax.rem(iz + h, NZ)} for h in Z_STEPS]
    p_peers = [
        plane(lax.rem(ix + h, NX), lax.rem(iy + g, NY))
        for h in (2, 1, 3, 0)
        for g in (2, 1, 3, 0)
        if h or g
    ]
    everyone = [sibling] + z_peers + p_peers

    barrier = pltpu.get_barrier_semaphore()
    for peer in everyone:
        pl.semaphore_signal(barrier, inc=1, device_id=peer, device_id_type=MESH)

    def remote(src, dst, ss, rs, peer):
        return pltpu.make_async_remote_copy(
            src_ref=src, dst_ref=dst, send_sem=ss, recv_sem=rs, device_id=peer, device_id_type=MESH
        )

    def in_copies(k):
        return [
            pltpu.make_async_copy(a.at[k], b.at[k], in_sem.at[i, k])
            for i, (a, b) in enumerate(((pos_hbm, pos), (low_hbm, low), (high_hbm, high)))
        ]

    small = [
        pltpu.make_async_copy(a, b, small_sem.at[i])
        for i, (a, b) in enumerate(
            ((drow_hbm, drow), (dcol_hbm, dcol), (upper_hbm, upper), (supp_hbm, supp))
        )
    ]
    for c in small:
        c.start()
    for j in range(K):
        for c in in_copies(lax.rem(ks + j, K)):
            c.start()

    for c in small:
        c.wait()

    column = (
        lax.broadcasted_iota(jnp.int32, (S, IL), 0) * (NZ * IL)
        + iz * IL
        + lax.broadcasted_iota(jnp.int32, (S, IL), 1)
    )
    for k in range(K):
        key[k] = jnp.where(column == att_c[k], att_r[k] - reg * RL, -1)

    @pl.loop(0, K)
    def _(k):
        d = drow[k]
        for r in range(RL):
            drow_b[k, pl.ds(r * S, S), :] = jnp.broadcast_to(d[:, r : r + 1], (S, IL))

    @pl.loop(0, RL)
    def _(r):
        u = upper[r].astype(F32)
        umat[r] = u
        amat[r] = supp[r].astype(F32)
        hmat[r] = BARRIER / u

    lane = lax.broadcasted_iota(jnp.int32, (S, IL), 1)

    @pl.loop(0, K)
    def _(j):
        k = lax.rem(ks + j, K)
        for c in in_copies(k):
            c.wait()
        zero = jnp.zeros((S, IL), F32)
        dc = dcol[k]
        ky = key[k]

        def body(b, carry):
            row_s, row_m, col_s, col_m = carry
            for i in range(2):
                r = b * 2 + i
                rows = pl.ds(pl.multiple_of(r * S, S), S)
                p = pos[k, r].astype(F32)
                dl = low[k, r].astype(F32)
                du = high[k, r].astype(F32)
                u = umat[r]
                hit = ky == r
                act = jnp.where(hit, 1.0, amat[r])
                om = 1.0 - p
                q = p * om
                den = dl * om + du * p
                rc = 1.0 / (q * den)
                qr = q * rc
                au = act * u
                high_s, low_s = split_pair(au * q * qr)
                sc = high_s.astype(F32) + low_s.astype(F32)
                g = hmat[r] * (om - p) * (den * rc) + jnp.where(hit, WEIGHT_ATTACK, 0.0) - dc
                m = au * (0.5 - p) + sc * (g - drow_b[k, rows, :])
                scal[k, rows, :] = sc
                grad[k, rows, :] = g
                col_s = col_s + sc
                col_m = col_m + m
                row_s = jnp.where(lane == r, jnp.sum(sc, axis=1, keepdims=True), row_s)
                row_m = jnp.where(lane == r, jnp.sum(m, axis=1, keepdims=True), row_m)
            return row_s, row_m, col_s, col_m

        row_s, row_m, col_s, col_m = lax.fori_loop(0, RL // 2, body, (zero, zero, zero, zero))
        part[k, 0] = row_s
        part[k, 1] = row_m
        part[k, 2] = col_s
        part[k, 3] = col_m

    pl.semaphore_wait(barrier, len(everyone))

    pair_part = remote(part.at[pl.ds(ks, KO)], part_x, pair_s.at[0], pair_r.at[0], sibling)
    pair_scal = remote(scal.at[pl.ds(ks, KO)], scal_x, pair_s.at[1], pair_r.at[1], sibling)
    pair_part.start()
    pair_scal.start()
    pair_part.wait()

    row_s = [part[kb + q, 0] + pltpu.roll(part_x[q, 0], RL, 1) for q in range(KO)]
    row_m = [part[kb + q, 1] + pltpu.roll(part_x[q, 1], RL, 1) for q in range(KO)]
    for q in range(KO):
        for i in range(2):
            ini_c1[q // 2, pl.ds(((q % 2) * 2 + i) * S, S), :] = part[kb + q, 2 + i] + part_x[q, 2 + i]
    packed_s, packed_m = pack(row_s), pack(row_m)
    ini_zs[0:48, :] = packed_s
    ini_zs[48:96, :] = packed_m

    def line_start(src, dst, ss, rs, first_x):
        for h in range(3):
            for half in range(2):
                along_x = (half == 0) == first_x
                peer = (x_peers if along_x else y_peers)[h]
                slot = ix if along_x else iy
                remote(src.at[half], dst.at[half, slot], ss.at[half], rs.at[half], peer).start()

    def line_finish(src, dst, ss, rs, first_x):
        for half in range(2):
            along_x = (half == 0) == first_x
            slot = ix if along_x else iy
            dst[half, slot] = src[half]
        for half in range(2):
            got = dst.at[half, pl.ds(0, 3)]
            c = remote(got, got, ss.at[half], rs.at[half], x_peers[0])
            c.wait_recv()
            c.wait_send()
        return [dst[half, 0] + dst[half, 1] + dst[half, 2] + dst[half, 3] for half in range(2)]

    def z_start(src, dst, ss, rs):
        for peer in z_peers:
            remote(src, dst.at[iz], ss, rs, peer).start()

    def z_finish(src, dst, ss, rs):
        dst[iz] = src[...]
        got = dst.at[pl.ds(0, NZ - 1)]
        c = remote(got, got, ss, rs, z_peers[0])
        c.wait_recv()
        c.wait_send()
        t = [dst[i] for i in range(NZ)]
        return ((t[0] + t[1]) + (t[2] + t[3])) + ((t[4] + t[5]) + (t[6] + t[7]))

    z_start(ini_zs, ini_zr, ini_s.at[0], ini_r.at[0])
    line_start(ini_c1, ini_c1r, ini_s.at[pl.ds(1, 2)], ini_r.at[pl.ds(1, 2)], True)

    pair_scal.wait()

    def build(t):
        q, s = t // S, lax.rem(t, S)
        own = scal[kb + q, pl.ds(s, RL, stride=S), :]
        other = scal_x[q, pl.ds(s, RL, stride=S), :]
        both = jnp.concatenate([own, other], axis=0)
        h, l = split_pair(both)
        mat_c[q, s, :, 0:IL] = h
        mat_c[q, s, :, IL : 2 * IL] = l
        turned = jnp.transpose(jnp.concatenate([both, jnp.zeros((32, IL), F32)], axis=0))
        h, l = split_pair(turned)
        mat_r[q, s, :, 0:128] = h
        mat_r[q, s, :, 128:256] = l

    HALF_BUILD = KO * S // 2
    pl.loop(0, HALF_BUILD)(build)

    halves = line_finish(ini_c1, ini_c1r, ini_s.at[pl.ds(1, 2)], ini_r.at[pl.ds(1, 2)], True)
    for half in range(2):
        ini_c2[half] = halves[half]
    line_start(ini_c2, ini_c2r, ini_s.at[pl.ds(3, 2)], ini_r.at[pl.ds(3, 2)], False)

    pl.loop(HALF_BUILD, KO * S)(build)

    total = z_finish(ini_zs, ini_zr, ini_s.at[0], ini_r.at[0])
    used = lane < 2 * RL
    for q, (d, m) in enumerate(zip(unpack(total[0:48]), unpack(total[48:96]))):
        d = d + SHIFT
        inv = jnp.where(used, 1.0 / d, 0.0)
        dia_r[q] = d
        inv_r[q] = inv
        hist_r[0, q] = m * inv
        cur_r[q] = m * inv
    halves = line_finish(ini_c2, ini_c2r, ini_s.at[pl.ds(3, 2)], ini_r.at[pl.ds(3, 2)], False)
    for q in range(KO):
        at = (q % 2) * 2 * S
        d = halves[q // 2][at : at + S] + SHIFT
        m = halves[q // 2][at + S : at + 2 * S]
        inv = 1.0 / d
        dia_c[q] = d
        inv_c[q] = inv
        hist_c[0, q] = m * inv
        cur_c[q] = m * inv

    size_of = lax.rem(lax.broadcasted_iota(jnp.int32, (3 * S, 256), 0), S)

    def couple_half(mat, vec, q, depth):
        left = split_three(vec)[:, 0:depth]
        acc = jnp.zeros((3 * S, 256), F32)
        for s in range(S):
            prod = lax.dot_general(
                left, mat[q, s], (((1,), (0,)), ((), ())), preferred_element_type=F32
            )
            acc = jnp.where(size_of == s, prod, acc)
        acc = acc[0:S] + acc[S : 2 * S] + acc[2 * S : 3 * S]
        return acc[:, 0:128] + acc[:, 128:256]

    sub8 = lax.broadcasted_iota(jnp.int32, (8, 128), 0)
    lane8 = lax.broadcasted_iota(jnp.int32, (8, 128), 1)

    def dot_tile(products):
        tile = jnp.zeros((8, 128), F32)
        for d, per in enumerate(products):
            for q in range(KO):
                t = jnp.sum(jnp.sum(per[q], axis=0, keepdims=True), axis=1, keepdims=True)
                tile = jnp.where((sub8 == q) & (lane8 == d), jnp.broadcast_to(t, (8, 128)), tile)
        return tile

    def p_start(n, tile):
        dps[n] = tile
        for peer in p_peers:
            remote(dps.at[n], dpr.at[n, ix * NY + iy], d_ss.at[n], d_rs.at[n], peer).start()

    def p_finish(n):
        dpr[n, ix * NY + iy] = dps[n]
        got = dpr.at[n, pl.ds(0, NX * NY - 1)]
        c = remote(got, got, d_ss.at[n], d_rs.at[n], p_peers[0])
        c.wait_recv()
        c.wait_send()
        t = [dpr[n, i] for i in range(NX * NY)]
        while len(t) > 1:
            t = [t[i] + t[i + 1] for i in range(0, len(t), 2)]
        return t[0]

    def zd_start(n, tile):
        dzs[n] = tile
        z_start(dzs.at[n], dzr.at[n], d_ss.at[3 + n], d_rs.at[3 + n])

    def zd_finish(n):
        return z_finish(dzs.at[n], dzr.at[n], d_ss.at[3 + n], d_rs.at[3 + n])

    def value(n, q, d):
        return scl[n, q : q + 1, d : d + 1]

    def first_step(hist, vec, cur):
        for q in range(KO):
            alpha = value(0, q, 0) / value(0, q, 1)
            z0, w1, w3 = vec[0, q], hist[3, q], hist[5, q]
            z1 = z0 - alpha * (z0 + w3)
            vec[1, q] = z1
            vec[2, q] = hist[0, q] - alpha * (z0 + w1)
            vec[3, q] = alpha * z0
            cur[q] = z1

    def after_round(j, hist, vec, cur, dia, start):
        @pl.when((j != 2) & (j != 5))
        def _():
            for q in range(KO):
                cur[q] = hist[j, q]

        @pl.when(j == 2)
        def _():
            for q in range(KO):
                z0 = hist[0, q] - hist[1, q] + hist[2, q]
                vec[0, q] = z0
                cur[q] = z0

        @pl.when(j == 3)
        def _():
            rz, cv = [], []
            for q in range(KO):
                z0 = vec[0, q]
                dz = dia[q] * z0
                rz.append(dz * hist[0, q])
                cv.append(dz * (z0 + hist[3, q]))
            start(0, dot_tile([rz, cv]))

        @pl.when(j == 6)
        def _():
            rz, zn, zp = [], [], []
            for q in range(KO):
                z1 = vec[1, q]
                dz = dia[q] * z1
                rz.append(dz * vec[2, q])
                zn.append(dz * (z1 + hist[6, q]))
                zp.append(dz * (vec[0, q] + hist[3, q]))
            start(1, dot_tile([rz, zn, zp]))

    @pl.loop(0, ROUNDS + 1)
    def _(j):
        now = lax.rem(j, 2)
        nxt = 1 - now

        def lines(n):
            at = pl.ds(n * 2, 2)
            return (
                (c1.at[n], c1r.at[n], c_ss.at[0, at], c_rs.at[0, at], True),
                (c2.at[n], c2r.at[n], c_ss.at[1, at], c_rs.at[1, at], False),
            )

        @pl.when(j > 0)
        def _():
            first, second = lines(now)
            halves = line_finish(*first)
            for half in range(2):
                c2[now, half] = halves[half]
            line_start(*second)
            total = z_finish(zs.at[now], zr.at[now], z_ss.at[now], z_rs.at[now])
            for q, t in enumerate(unpack(total)):
                hist_r[j, q] = t * inv_r[q]

            @pl.when(j == 5)
            def _():
                scl[0] = zd_finish(0) + p_finish(0)
                first_step(hist_r, vec_r, cur_r)

            after_round(j, hist_r, vec_r, cur_r, dia_r, p_start)

        @pl.when(j < ROUNDS)
        def _():
            for q in range(KO):
                c1[nxt, q // 2, (q % 2) * S : (q % 2 + 1) * S, :] = couple_half(mat_c, cur_r[q], q, 96)
            line_start(*lines(nxt)[0])

        @pl.when(j > 0)
        def _():
            halves = line_finish(*lines(now)[1])
            for q in range(KO):
                at = (q % 2) * S
                hist_c[j, q] = halves[q // 2][at : at + S] * inv_c[q]

            @pl.when(j == 5)
            def _():
                first_step(hist_c, vec_c, cur_c)

            after_round(j, hist_c, vec_c, cur_c, dia_c, zd_start)

        @pl.when(j < ROUNDS)
        def _():
            zs[nxt] = pack([couple_half(mat_r, cur_c[q], q, 128) for q in range(KO)])
            z_start(zs.at[nxt], zr.at[nxt], z_ss.at[nxt], z_rs.at[nxt])

    scl[1] = zd_finish(1) + p_finish(1)
    steps = []
    for q in range(KO):
        beta = value(1, q, 0) / value(0, q, 0)
        curv = value(1, q, 1) + 2.0 * beta * value(1, q, 2) + beta * beta * value(0, q, 1)
        steps.append((beta, curv, value(1, q, 0) / curv))

    def second_step(hist, vec, cur, dia):
        rz, zp, zz = [], [], []
        for q in range(KO):
            beta, _, alpha = steps[q]
            p1 = vec[1, q] + beta * vec[0, q]
            np1 = p1 + hist[6, q] + beta * hist[3, q]
            z2 = vec[1, q] - alpha * (p1 + hist[8, q] + beta * hist[5, q])
            g2 = vec[2, q] - alpha * np1
            vec[3, q] = vec[3, q] + alpha * p1
            vec[4, q] = p1
            cur[q] = z2
            dz = dia[q] * z2
            rz.append(dz * g2)
            zp.append(dz * np1)
            zz.append(dz * z2)
        return [rz, zp, zz]

    dots_c = second_step(hist_c, vec_c, cur_c, dia_c)
    dots_r = second_step(hist_r, vec_r, cur_r, dia_r)
    cross = [2.0 * couple_half(mat_c, cur_r[q], q, 96) * cur_c[q] for q in range(KO)]
    zd_start(2, dot_tile(dots_c + [cross]))
    tile_r = dot_tile(dots_r)
    tile_c = zd_finish(2)
    p_start(2, tile_r + jnp.where(lane8 == 3, tile_c, 0.0))
    scl[2] = p_finish(2) + jnp.where(lane8 < 3, tile_c, 0.0)
    for q in range(KO):
        _, curv1, _ = steps[q]
        rz2 = value(2, q, 0)
        beta = rz2 / value(1, q, 0)
        curv = (
            value(2, q, 2) + value(2, q, 3) + 2.0 * beta * value(2, q, 1) + beta * beta * curv1
        )
        alpha = rz2 / curv
        for i, (vec, cur) in enumerate(((vec_r, cur_r), (vec_c, cur_c))):
            y = vec[3, q] + alpha * (cur[q] + beta * vec[4, q])
            if i == 0:
                fin_r[kb + q] = y
                y = pltpu.roll(y, 128 - RL, 1)
            else:
                col_out[kb + q] = y
            fin[i, q] = y
    swap = remote(fin, fin_x, pair_s.at[2], pair_r.at[2], sibling)
    swap.start()
    swap.wait()
    for q in range(KO):
        fin_r[ks + q] = fin_x[0, q]
        col_out[ks + q] = fin_x[1, q]

    @pl.loop(0, K)
    def _(k):
        y = fin_r[k]
        row_out[k] = y
        y = y + drow[k]
        c = col_out[k]
        for r in range(RL):
            rows = pl.ds(r * S, S)
            t = jnp.broadcast_to(y[:, r : r + 1], (S, IL)) + (c - grad[k, rows, :])
            cell[k, r] = (scal[k, rows, :] * t).astype(BF16)
        pltpu.make_async_copy(cell.at[k], cell_hbm.at[k], out_sem.at[k]).start()

    for k in range(K):
        pltpu.make_async_copy(cell.at[k], cell_hbm.at[k], out_sem.at[k]).wait()


def local(pos, low, high, upper, supp, att_r, att_c, drow, dcol):
    turned = jnp.pad(jnp.transpose(drow, (0, 2, 1)), ((0, 0), (0, 0), (0, 128 - RL)))
    V, DMA = pltpu.VMEM, pltpu.SemaphoreType.DMA
    cells = (K, RL, S, IL)
    scratch = [
        V(cells, BF16), V(cells, BF16), V(cells, BF16),
        V((RL, S, IL), jnp.int32), V((RL, S, IL), jnp.int32),
        V((K, S, 128), F32), V((K, S, IL), F32),
        DMA((3, K)), DMA((4,)),
        V((K, RL * S, IL), F32), V((KO, RL * S, IL), F32), V((K, RL * S, IL), F32),
        V((K, RL * S, IL), F32),
        V((RL, S, IL), F32), V((RL, S, IL), F32), V((RL, S, IL), F32),
        V((K, S, IL), jnp.int32),
        V((K, 4, S, 128), F32), V((KO, 4, S, 128), F32), DMA((3,)), DMA((3,)),
        V((KO, S, 2 * RL, 2 * IL), BF16), V((KO, S, IL, 256), BF16),
        V((96, 128), F32), V((NZ, 96, 128), F32),
        V((2, 64, 128), F32), V((2, 4, 64, 128), F32), V((2, 64, 128), F32), V((2, 4, 64, 128), F32),
        DMA((5,)), DMA((5,)),
        V((2, 48, 128), F32), V((2, NZ, 48, 128), F32), DMA((2,)), DMA((2,)),
        V((2, 2, 32, 128), F32), V((2, 2, 4, 32, 128), F32),
        V((2, 2, 32, 128), F32), V((2, 2, 4, 32, 128), F32),
        DMA((2, 4)), DMA((2, 4)),
        V((3, 8, 128), F32), V((3, NZ, 8, 128), F32), V((3, 8, 128), F32), V((3, NX * NY, 8, 128), F32),
        DMA((6,)), DMA((6,)),
        V((ROUNDS + 1, KO, S, 128), F32), V((ROUNDS + 1, KO, S, 128), F32),
        V((KO, S, 128), F32), V((KO, S, 128), F32), V((KO, S, 128), F32), V((KO, S, 128), F32),
        V((5, KO, S, 128), F32), V((5, KO, S, 128), F32),
        V((KO, S, 128), F32), V((KO, S, 128), F32),
        V((3, 8, 128), F32),
        V((2, KO, S, 128), F32), V((2, KO, S, 128), F32), V((K, S, 128), F32),
        V(cells, BF16), DMA((K,)),
    ]
    any_spec = pl.BlockSpec(memory_space=pl.ANY)
    smem_spec = pl.BlockSpec(memory_space=pltpu.SMEM)
    vmem_spec = pl.BlockSpec(memory_space=pltpu.VMEM)
    cell, row, col = pl.pallas_call(
        kernel,
        out_shape=(
            jax.ShapeDtypeStruct(cells, BF16),
            jax.ShapeDtypeStruct((K, S, 128), F32),
            jax.ShapeDtypeStruct((K, S, IL), F32),
        ),
        in_specs=[any_spec] * 5 + [smem_spec] * 2 + [any_spec] * 2,
        out_specs=(any_spec, vmem_spec, vmem_spec),
        scratch_shapes=scratch,
        compiler_params=pltpu.CompilerParams(
            collective_id=0, has_side_effects=True, vmem_limit_bytes=50 * 1024 * 1024
        ),
    )(pos, low, high, upper, supp, att_r, att_c, turned, dcol)
    return cell, jnp.transpose(row[:, :, :RL], (0, 2, 1)), col


def solution(mesh):
    cells = P(None, "region", None, "industry")
    return jax.shard_map(
        local,
        mesh=mesh,
        in_specs=(
            cells, cells, cells,
            P("region", None, "industry"), P("region", None, "industry"),
            P(), P(), P(None, "region", None), P(None, None, "industry"),
        ),
        out_specs=(cells, P(None, "region", None), P(None, None, "industry")),
        check_vma=False,
    )
```

```python
import jax
import jax.numpy as jnp
from jax import lax
from jax.experimental import pallas as pl
from jax.experimental.pallas import tpu as pltpu
from jax.sharding import PartitionSpec as P

MESH = pl.DeviceIdType.MESH
F32 = jnp.float32
BF16 = jnp.bfloat16
K, RL, S, IL = 8, 48, 16, 128
KO = 4
NZ, NX, NY = 8, 4, 4
ROUNDS = 8
WEIGHT_ATTACK, BARRIER, SHIFT = 8.0, 0.5, 1.0
Z_STEPS = (4, 3, 5, 2, 6, 1, 7)
LINE_STEPS = (2, 1, 3)


def split_pair(x):
    high = x.astype(BF16)
    low = (x - high.astype(F32)).astype(BF16)
    return high, low


def split_three(x):
    high = x.astype(BF16)
    rest = x - high.astype(F32)
    mid = rest.astype(BF16)
    low = (rest - mid.astype(F32)).astype(BF16)
    return jnp.concatenate([high, mid, low], axis=0)


def pack(rows):
    tiles = [rows[q][8 * h : 8 * h + 8] for q in range(KO) for h in range(2)]
    lane = lax.broadcasted_iota(jnp.int32, (8, 128), 1)
    packed = []
    for i in range(6):
        spare = pltpu.roll(tiles[6 + i // 3], 96 - 32 * (i % 3), 1)
        packed.append(jnp.where(lane < 96, tiles[i], spare))
    return jnp.concatenate(packed, axis=0)


def unpack(packed):
    lane = lax.broadcasted_iota(jnp.int32, (8, 128), 1)
    zero = jnp.zeros((8, 128), F32)
    m = [packed[8 * i : 8 * i + 8] for i in range(6)]
    tiles = [jnp.where(lane < 96, x, zero) for x in m]
    for g in range(2):
        a = pltpu.roll(m[3 * g], 32, 1)
        b = pltpu.roll(m[3 * g + 1], 64, 1)
        c = pltpu.roll(m[3 * g + 2], 96, 1)
        tiles.append(
            jnp.where(lane < 32, a, jnp.where(lane < 64, b, jnp.where(lane < 96, c, zero)))
        )
    return [jnp.concatenate([tiles[2 * q], tiles[2 * q + 1]], axis=0) for q in range(KO)]


def kernel(
    pos_hbm, low_hbm, high_hbm, upper_hbm, supp_hbm, att_r, att_c, drow_hbm, dcol_hbm,
    cell_hbm, row_out, col_out,
    pos, low, high, upper, supp, drow, dcol, in_sem, small_sem,
    scal, scal_x, grad, drow_b, umat, amat, hmat, key, part, part_x, pair_s, pair_r,
    mat_c, mat_r,
    ini_zs, ini_zr, ini_c1, ini_c1r, ini_c2, ini_c2r, ini_s, ini_r,
    zs, zr, z_ss, z_rs,
    c1, c1r, c2, c2r, c_ss, c_rs,
    dzs, dzr, dps, dpr, d_ss, d_rs,
    hist_r, hist_c, dia_r, dia_c, inv_r, inv_c, vec_r, vec_c, cur_r, cur_c, scl,
    fin, fin_x, fin_r, cell, out_sem,
):
    reg = lax.axis_index("region")
    iz = lax.axis_index("industry")
    core = lax.rem(reg, 2)
    iy = lax.rem(reg // 2, NY)
    ix = reg // (2 * NY)
    kb = core * KO
    ks = KO - kb
    sibling = {"region": reg + 1 - 2 * core}

    def plane(x, y):
        return {"region": (x * NY + y) * 2 + core}

    x_peers = [plane(lax.rem(ix + h, NX), iy) for h in LINE_STEPS]
    y_peers = [plane(ix, lax.rem(iy + h, NY)) for h in LINE_STEPS]
    z_peers = [{"industry": lax.rem(iz + h, NZ)} for h in Z_STEPS]
    p_peers = [
        plane(lax.rem(ix + h, NX), lax.rem(iy + g, NY))
        for h in (2, 1, 3, 0)
        for g in (2, 1, 3, 0)
        if h or g
    ]
    everyone = [sibling] + z_peers + p_peers

    barrier = pltpu.get_barrier_semaphore()
    for peer in everyone:
        pl.semaphore_signal(barrier, inc=1, device_id=peer, device_id_type=MESH)

    def remote(src, dst, ss, rs, peer):
        return pltpu.make_async_remote_copy(
            src_ref=src, dst_ref=dst, send_sem=ss, recv_sem=rs, device_id=peer, device_id_type=MESH
        )

    def in_copies(k):
        return [
            pltpu.make_async_copy(a.at[k], b.at[k], in_sem.at[i, k])
            for i, (a, b) in enumerate(((pos_hbm, pos), (low_hbm, low), (high_hbm, high)))
        ]

    small = [
        pltpu.make_async_copy(a, b, small_sem.at[i])
        for i, (a, b) in enumerate(
            ((drow_hbm, drow), (dcol_hbm, dcol), (upper_hbm, upper), (supp_hbm, supp))
        )
    ]
    for c in small:
        c.start()
    for j in range(K):
        for c in in_copies(lax.rem(ks + j, K)):
            c.start()

    for c in small:
        c.wait()

    column = (
        lax.broadcasted_iota(jnp.int32, (S, IL), 0) * (NZ * IL)
        + iz * IL
        + lax.broadcasted_iota(jnp.int32, (S, IL), 1)
    )
    for k in range(K):
        key[k] = jnp.where(column == att_c[k], att_r[k] - reg * RL, -1)

    @pl.loop(0, K)
    def _(k):
        d = drow[k]
        for r in range(RL):
            drow_b[k, pl.ds(r * S, S), :] = jnp.broadcast_to(d[:, r : r + 1], (S, IL))

    @pl.loop(0, RL)
    def _(r):
        u = upper[r].astype(F32)
        umat[r] = u
        amat[r] = supp[r].astype(F32)
        hmat[r] = BARRIER / u

    lane = lax.broadcasted_iota(jnp.int32, (S, IL), 1)

    @pl.loop(0, K)
    def _(j):
        k = lax.rem(ks + j, K)
        for c in in_copies(k):
            c.wait()
        zero = jnp.zeros((S, IL), F32)
        dc = dcol[k]
        ky = key[k]

        row_s, row_m, col_s, col_m = zero, zero, zero, zero
        if True:
            for r in range(RL):
                rows = pl.ds(r * S, S)
                p = pos[k, r].astype(F32)
                dl = low[k, r].astype(F32)
                du = high[k, r].astype(F32)
                u = umat[r]
                hit = ky == r
                act = jnp.where(hit, 1.0, amat[r])
                om = 1.0 - p
                q = p * om
                den = dl * om + du * p
                rc = 1.0 / (q * den)
                qr = q * rc
                au = act * u
                high_s, low_s = split_pair(au * q * qr)
                sc = high_s.astype(F32) + low_s.astype(F32)
                g = hmat[r] * (om - p) * (den * rc) + jnp.where(hit, WEIGHT_ATTACK, 0.0) - dc
                m = au * (0.5 - p) + sc * (g - drow_b[k, rows, :])
                scal[k, rows, :] = sc
                grad[k, rows, :] = g
                col_s = col_s + sc
                col_m = col_m + m
                row_s = jnp.where(lane == r, jnp.sum(sc, axis=1, keepdims=True), row_s)
                row_m = jnp.where(lane == r, jnp.sum(m, axis=1, keepdims=True), row_m)
        part[k, 0] = row_s
        part[k, 1] = row_m
        part[k, 2] = col_s
        part[k, 3] = col_m

    pl.semaphore_wait(barrier, len(everyone))

    pair_part = remote(part.at[pl.ds(ks, KO)], part_x, pair_s.at[0], pair_r.at[0], sibling)
    pair_scal = remote(scal.at[pl.ds(ks, KO)], scal_x, pair_s.at[1], pair_r.at[1], sibling)
    pair_part.start()
    pair_scal.start()
    pair_part.wait()

    row_s = [part[kb + q, 0] + pltpu.roll(part_x[q, 0], RL, 1) for q in range(KO)]
    row_m = [part[kb + q, 1] + pltpu.roll(part_x[q, 1], RL, 1) for q in range(KO)]
    for q in range(KO):
        for i in range(2):
            ini_c1[q // 2, pl.ds(((q % 2) * 2 + i) * S, S), :] = part[kb + q, 2 + i] + part_x[q, 2 + i]
    packed_s, packed_m = pack(row_s), pack(row_m)
    ini_zs[0:48, :] = packed_s
    ini_zs[48:96, :] = packed_m

    def line_start(src, dst, ss, rs, first_x):
        for h in range(3):
            for half in range(2):
                along_x = (half == 0) == first_x
                peer = (x_peers if along_x else y_peers)[h]
                slot = ix if along_x else iy
                remote(src.at[half], dst.at[half, slot], ss.at[half], rs.at[half], peer).start()

    def line_finish(src, dst, ss, rs, first_x):
        for half in range(2):
            along_x = (half == 0) == first_x
            slot = ix if along_x else iy
            dst[half, slot] = src[half]
        for half in range(2):
            got = dst.at[half, pl.ds(0, 3)]
            c = remote(got, got, ss.at[half], rs.at[half], x_peers[0])
            c.wait_recv()
            c.wait_send()
        return [dst[half, 0] + dst[half, 1] + dst[half, 2] + dst[half, 3] for half in range(2)]

    def z_start(src, dst, ss, rs):
        for peer in z_peers:
            remote(src, dst.at[iz], ss, rs, peer).start()

    def z_finish(src, dst, ss, rs):
        dst[iz] = src[...]
        got = dst.at[pl.ds(0, NZ - 1)]
        c = remote(got, got, ss, rs, z_peers[0])
        c.wait_recv()
        c.wait_send()
        t = [dst[i] for i in range(NZ)]
        return ((t[0] + t[1]) + (t[2] + t[3])) + ((t[4] + t[5]) + (t[6] + t[7]))

    z_start(ini_zs, ini_zr, ini_s.at[0], ini_r.at[0])
    line_start(ini_c1, ini_c1r, ini_s.at[pl.ds(1, 2)], ini_r.at[pl.ds(1, 2)], True)

    pair_scal.wait()

    def build(t):
        q, s = t // S, lax.rem(t, S)
        own = scal[kb + q, pl.ds(s, RL, stride=S), :]
        other = scal_x[q, pl.ds(s, RL, stride=S), :]
        both = jnp.concatenate([own, other], axis=0)
        h, l = split_pair(both)
        mat_c[q, s, :, 0:IL] = h
        mat_c[q, s, :, IL : 2 * IL] = l
        turned = jnp.transpose(jnp.concatenate([both, jnp.zeros((32, IL), F32)], axis=0))
        h, l = split_pair(turned)
        mat_r[q, s, :, 0:128] = h
        mat_r[q, s, :, 128:256] = l

    HALF_BUILD = KO * S // 2
    pl.loop(0, HALF_BUILD)(build)

    halves = line_finish(ini_c1, ini_c1r, ini_s.at[pl.ds(1, 2)], ini_r.at[pl.ds(1, 2)], True)
    for half in range(2):
        ini_c2[half] = halves[half]
    line_start(ini_c2, ini_c2r, ini_s.at[pl.ds(3, 2)], ini_r.at[pl.ds(3, 2)], False)

    pl.loop(HALF_BUILD, KO * S)(build)

    total = z_finish(ini_zs, ini_zr, ini_s.at[0], ini_r.at[0])
    used = lane < 2 * RL
    for q, (d, m) in enumerate(zip(unpack(total[0:48]), unpack(total[48:96]))):
        d = d + SHIFT
        inv = jnp.where(used, 1.0 / d, 0.0)
        dia_r[q] = d
        inv_r[q] = inv
        hist_r[0, q] = m * inv
        cur_r[q] = m * inv
    halves = line_finish(ini_c2, ini_c2r, ini_s.at[pl.ds(3, 2)], ini_r.at[pl.ds(3, 2)], False)
    for q in range(KO):
        at = (q % 2) * 2 * S
        d = halves[q // 2][at : at + S] + SHIFT
        m = halves[q // 2][at + S : at + 2 * S]
        inv = 1.0 / d
        dia_c[q] = d
        inv_c[q] = inv
        hist_c[0, q] = m * inv
        cur_c[q] = m * inv

    size_of = lax.rem(lax.broadcasted_iota(jnp.int32, (3 * S, 256), 0), S)

    def couple_half(mat, vec, q, depth):
        left = split_three(vec)[:, 0:depth]
        acc = jnp.zeros((3 * S, 256), F32)
        for s in range(S):
            prod = lax.dot_general(
                left, mat[q, s], (((1,), (0,)), ((), ())), preferred_element_type=F32
            )
            acc = jnp.where(size_of == s, prod, acc)
        acc = acc[0:S] + acc[S : 2 * S] + acc[2 * S : 3 * S]
        return acc[:, 0:128] + acc[:, 128:256]

    sub8 = lax.broadcasted_iota(jnp.int32, (8, 128), 0)
    lane8 = lax.broadcasted_iota(jnp.int32, (8, 128), 1)

    def dot_tile(products):
        tile = jnp.zeros((8, 128), F32)
        for d, per in enumerate(products):
            for q in range(KO):
                t = jnp.sum(jnp.sum(per[q], axis=0, keepdims=True), axis=1, keepdims=True)
                tile = jnp.where((sub8 == q) & (lane8 == d), jnp.broadcast_to(t, (8, 128)), tile)
        return tile

    def p_start(n, tile):
        dps[n] = tile
        for peer in p_peers:
            remote(dps.at[n], dpr.at[n, ix * NY + iy], d_ss.at[n], d_rs.at[n], peer).start()

    def p_finish(n):
        dpr[n, ix * NY + iy] = dps[n]
        got = dpr.at[n, pl.ds(0, NX * NY - 1)]
        c = remote(got, got, d_ss.at[n], d_rs.at[n], p_peers[0])
        c.wait_recv()
        c.wait_send()
        t = [dpr[n, i] for i in range(NX * NY)]
        while len(t) > 1:
            t = [t[i] + t[i + 1] for i in range(0, len(t), 2)]
        return t[0]

    def zd_start(n, tile):
        dzs[n] = tile
        z_start(dzs.at[n], dzr.at[n], d_ss.at[3 + n], d_rs.at[3 + n])

    def zd_finish(n):
        return z_finish(dzs.at[n], dzr.at[n], d_ss.at[3 + n], d_rs.at[3 + n])

    def value(n, q, d):
        return scl[n, q : q + 1, d : d + 1]

    def first_step(hist, vec, cur):
        for q in range(KO):
            alpha = value(0, q, 0) / value(0, q, 1)
            z0, w1, w3 = vec[0, q], hist[3, q], hist[5, q]
            z1 = z0 - alpha * (z0 + w3)
            vec[1, q] = z1
            vec[2, q] = hist[0, q] - alpha * (z0 + w1)
            vec[3, q] = alpha * z0
            cur[q] = z1

    def after_round(j, hist, vec, cur, dia, start):
        @pl.when((j != 2) & (j != 5))
        def _():
            for q in range(KO):
                cur[q] = hist[j, q]

        @pl.when(j == 2)
        def _():
            for q in range(KO):
                z0 = hist[0, q] - hist[1, q] + hist[2, q]
                vec[0, q] = z0
                cur[q] = z0

        @pl.when(j == 3)
        def _():
            rz, cv = [], []
            for q in range(KO):
                z0 = vec[0, q]
                dz = dia[q] * z0
                rz.append(dz * hist[0, q])
                cv.append(dz * (z0 + hist[3, q]))
            start(0, dot_tile([rz, cv]))

        @pl.when(j == 6)
        def _():
            rz, zn, zp = [], [], []
            for q in range(KO):
                z1 = vec[1, q]
                dz = dia[q] * z1
                rz.append(dz * vec[2, q])
                zn.append(dz * (z1 + hist[6, q]))
                zp.append(dz * (vec[0, q] + hist[3, q]))
            start(1, dot_tile([rz, zn, zp]))

    @pl.loop(0, ROUNDS + 1)
    def _(j):
        now = lax.rem(j, 2)
        nxt = 1 - now

        def lines(n):
            at = pl.ds(n * 2, 2)
            return (
                (c1.at[n], c1r.at[n], c_ss.at[0, at], c_rs.at[0, at], True),
                (c2.at[n], c2r.at[n], c_ss.at[1, at], c_rs.at[1, at], False),
            )

        @pl.when(j > 0)
        def _():
            first, second = lines(now)
            halves = line_finish(*first)
            for half in range(2):
                c2[now, half] = halves[half]
            line_start(*second)
            total = z_finish(zs.at[now], zr.at[now], z_ss.at[now], z_rs.at[now])
            for q, t in enumerate(unpack(total)):
                hist_r[j, q] = t * inv_r[q]

            @pl.when(j == 5)
            def _():
                scl[0] = zd_finish(0) + p_finish(0)
                first_step(hist_r, vec_r, cur_r)

            after_round(j, hist_r, vec_r, cur_r, dia_r, p_start)

        @pl.when(j < ROUNDS)
        def _():
            for q in range(KO):
                c1[nxt, q // 2, (q % 2) * S : (q % 2 + 1) * S, :] = couple_half(mat_c, cur_r[q], q, 96)
            line_start(*lines(nxt)[0])

        @pl.when(j > 0)
        def _():
            halves = line_finish(*lines(now)[1])
            for q in range(KO):
                at = (q % 2) * S
                hist_c[j, q] = halves[q // 2][at : at + S] * inv_c[q]

            @pl.when(j == 5)
            def _():
                first_step(hist_c, vec_c, cur_c)

            after_round(j, hist_c, vec_c, cur_c, dia_c, zd_start)

        @pl.when(j < ROUNDS)
        def _():
            zs[nxt] = pack([couple_half(mat_r, cur_c[q], q, 128) for q in range(KO)])
            z_start(zs.at[nxt], zr.at[nxt], z_ss.at[nxt], z_rs.at[nxt])

    scl[1] = zd_finish(1) + p_finish(1)
    steps = []
    for q in range(KO):
        beta = value(1, q, 0) / value(0, q, 0)
        curv = value(1, q, 1) + 2.0 * beta * value(1, q, 2) + beta * beta * value(0, q, 1)
        steps.append((beta, curv, value(1, q, 0) / curv))

    def second_step(hist, vec, cur, dia):
        rz, zp, zz = [], [], []
        for q in range(KO):
            beta, _, alpha = steps[q]
            p1 = vec[1, q] + beta * vec[0, q]
            np1 = p1 + hist[6, q] + beta * hist[3, q]
            z2 = vec[1, q] - alpha * (p1 + hist[8, q] + beta * hist[5, q])
            g2 = vec[2, q] - alpha * np1
            vec[3, q] = vec[3, q] + alpha * p1
            vec[4, q] = p1
            cur[q] = z2
            dz = dia[q] * z2
            rz.append(dz * g2)
            zp.append(dz * np1)
            zz.append(dz * z2)
        return [rz, zp, zz]

    dots_c = second_step(hist_c, vec_c, cur_c, dia_c)
    dots_r = second_step(hist_r, vec_r, cur_r, dia_r)
    cross = [2.0 * couple_half(mat_c, cur_r[q], q, 96) * cur_c[q] for q in range(KO)]
    zd_start(2, dot_tile(dots_c + [cross]))
    tile_r = dot_tile(dots_r)
    tile_c = zd_finish(2)
    p_start(2, tile_r + jnp.where(lane8 == 3, tile_c, 0.0))
    scl[2] = p_finish(2) + jnp.where(lane8 < 3, tile_c, 0.0)
    for q in range(KO):
        _, curv1, _ = steps[q]
        rz2 = value(2, q, 0)
        beta = rz2 / value(1, q, 0)
        curv = (
            value(2, q, 2) + value(2, q, 3) + 2.0 * beta * value(2, q, 1) + beta * beta * curv1
        )
        alpha = rz2 / curv
        for i, (vec, cur) in enumerate(((vec_r, cur_r), (vec_c, cur_c))):
            y = vec[3, q] + alpha * (cur[q] + beta * vec[4, q])
            if i == 0:
                fin_r[kb + q] = y
                y = pltpu.roll(y, 128 - RL, 1)
            else:
                col_out[kb + q] = y
            fin[i, q] = y
    swap = remote(fin, fin_x, pair_s.at[2], pair_r.at[2], sibling)
    swap.start()
    swap.wait()
    for q in range(KO):
        fin_r[ks + q] = fin_x[0, q]
        col_out[ks + q] = fin_x[1, q]

    @pl.loop(0, K)
    def _(k):
        y = fin_r[k]
        row_out[k] = y
        y = y + drow[k]
        c = col_out[k]
        for r in range(RL):
            rows = pl.ds(r * S, S)
            t = jnp.broadcast_to(y[:, r : r + 1], (S, IL)) + (c - grad[k, rows, :])
            cell[k, r] = (scal[k, rows, :] * t).astype(BF16)
        pltpu.make_async_copy(cell.at[k], cell_hbm.at[k], out_sem.at[k]).start()

    for k in range(K):
        pltpu.make_async_copy(cell.at[k], cell_hbm.at[k], out_sem.at[k]).wait()


def local(pos, low, high, upper, supp, att_r, att_c, drow, dcol):
    turned = jnp.pad(jnp.transpose(drow, (0, 2, 1)), ((0, 0), (0, 0), (0, 128 - RL)))
    V, DMA = pltpu.VMEM, pltpu.SemaphoreType.DMA
    cells = (K, RL, S, IL)
    scratch = [
        V(cells, BF16), V(cells, BF16), V(cells, BF16),
        V((RL, S, IL), jnp.int32), V((RL, S, IL), jnp.int32),
        V((K, S, 128), F32), V((K, S, IL), F32),
        DMA((3, K)), DMA((4,)),
        V((K, RL * S, IL), F32), V((KO, RL * S, IL), F32), V((K, RL * S, IL), F32),
        V((K, RL * S, IL), F32),
        V((RL, S, IL), F32), V((RL, S, IL), F32), V((RL, S, IL), F32),
        V((K, S, IL), jnp.int32),
        V((K, 4, S, 128), F32), V((KO, 4, S, 128), F32), DMA((3,)), DMA((3,)),
        V((KO, S, 2 * RL, 2 * IL), BF16), V((KO, S, IL, 256), BF16),
        V((96, 128), F32), V((NZ, 96, 128), F32),
        V((2, 64, 128), F32), V((2, 4, 64, 128), F32), V((2, 64, 128), F32), V((2, 4, 64, 128), F32),
        DMA((5,)), DMA((5,)),
        V((2, 48, 128), F32), V((2, NZ, 48, 128), F32), DMA((2,)), DMA((2,)),
        V((2, 2, 32, 128), F32), V((2, 2, 4, 32, 128), F32),
        V((2, 2, 32, 128), F32), V((2, 2, 4, 32, 128), F32),
        DMA((2, 4)), DMA((2, 4)),
        V((3, 8, 128), F32), V((3, NZ, 8, 128), F32), V((3, 8, 128), F32), V((3, NX * NY, 8, 128), F32),
        DMA((6,)), DMA((6,)),
        V((ROUNDS + 1, KO, S, 128), F32), V((ROUNDS + 1, KO, S, 128), F32),
        V((KO, S, 128), F32), V((KO, S, 128), F32), V((KO, S, 128), F32), V((KO, S, 128), F32),
        V((5, KO, S, 128), F32), V((5, KO, S, 128), F32),
        V((KO, S, 128), F32), V((KO, S, 128), F32),
        V((3, 8, 128), F32),
        V((2, KO, S, 128), F32), V((2, KO, S, 128), F32), V((K, S, 128), F32),
        V(cells, BF16), DMA((K,)),
    ]
    any_spec = pl.BlockSpec(memory_space=pl.ANY)
    hbm_spec = pl.BlockSpec(memory_space=pltpu.HBM)
    smem_spec = pl.BlockSpec(memory_space=pltpu.SMEM)
    vmem_spec = pl.BlockSpec(memory_space=pltpu.VMEM)
    cell, row, col = pl.pallas_call(
        kernel,
        out_shape=(
            jax.ShapeDtypeStruct(cells, BF16),
            jax.ShapeDtypeStruct((K, S, 128), F32),
            jax.ShapeDtypeStruct((K, S, IL), F32),
        ),
        in_specs=[hbm_spec] * 5 + [smem_spec] * 2 + [hbm_spec] * 2,
        out_specs=(any_spec, vmem_spec, vmem_spec),
        scratch_shapes=scratch,
        compiler_params=pltpu.CompilerParams(
            collective_id=0, has_side_effects=True, vmem_limit_bytes=50 * 1024 * 1024
        ),
    )(pos, low, high, upper, supp, att_r, att_c, turned, dcol)
    return cell, jnp.transpose(row[:, :, :RL], (0, 2, 1)), col


def solution(mesh):
    cells = P(None, "region", None, "industry")
    return jax.shard_map(
        local,
        mesh=mesh,
        in_specs=(
            cells, cells, cells,
            P("region", None, "industry"), P("region", None, "industry"),
            P(), P(), P(None, "region", None), P(None, None, "industry"),
        ),
        out_specs=(cells, P(None, "region", None), P(None, None, "industry")),
        check_vma=False,
    )
```

```python
import jax
import jax.numpy as jnp
from jax import lax
from jax.experimental import pallas as pl
from jax.experimental.pallas import tpu as pltpu
from jax.sharding import PartitionSpec as P

MESH = pl.DeviceIdType.MESH
F32 = jnp.float32
BF16 = jnp.bfloat16
K, RL, S, IL = 8, 48, 16, 128
KO = 4
NZ, NX, NY = 8, 4, 4
ROUNDS = 8
VL = 50
WEIGHT_ATTACK, BARRIER, SHIFT = 8.0, 0.5, 1.0
Z_STEPS = (4, 3, 5, 2, 6, 1, 7)
LINE_STEPS = (2, 1, 3)


def split_pair(x):
    high = x.astype(BF16)
    low = (x - high.astype(F32)).astype(BF16)
    return high, low


def split_three(x):
    high = x.astype(BF16)
    rest = x - high.astype(F32)
    mid = rest.astype(BF16)
    low = (rest - mid.astype(F32)).astype(BF16)
    return jnp.concatenate([high, mid, low], axis=0)


def pack(rows):
    tiles = [x[8 * h : 8 * h + 8] for x in rows for h in range(2)]
    lane = lax.broadcasted_iota(jnp.int32, (8, 128), 1)
    packed = [
        jnp.where(lane < 96, tiles[i], pltpu.roll(tiles[3], 96 - 32 * i, 1)) for i in range(3)
    ]
    return jnp.concatenate(packed, axis=0)


def unpack(packed):
    lane = lax.broadcasted_iota(jnp.int32, (8, 128), 1)
    zero = jnp.zeros((8, 128), F32)
    m = [packed[8 * i : 8 * i + 8] for i in range(3)]
    tiles = [jnp.where(lane < 96, x, zero) for x in m]
    a, b, c = (pltpu.roll(m[i], 32 + 32 * i, 1) for i in range(3))
    tiles.append(
        jnp.where(lane < 32, a, jnp.where(lane < 64, b, jnp.where(lane < 96, c, zero)))
    )
    return [jnp.concatenate([tiles[2 * q], tiles[2 * q + 1]], axis=0) for q in range(2)]


def kernel(
    pos_hbm, low_hbm, high_hbm, upper_hbm, supp_hbm, att_r, att_c, drow_hbm, dcol_hbm,
    cell_hbm, row_out, col_out,
    pos, low, high, upper, supp, drow, dcol, in_sem, small_sem,
    scal, scal_x, grad, drow_b, umat, amat, hmat, key, part, part_x, pair_s, pair_r,
    mat_c, mat_r,
    ini_zs, ini_zr, ini_as, ini_ar, ini_c1, ini_c1r, ini_c2, ini_c2r, ini_s, ini_r,
    zs, zr, z_ss, z_rs,
    c1, c1r, c2, c2r, c_ss, c_rs,
    dzs, dzr, dps, dpr, dfr, d_ss, d_rs,
    hist_r, hist_c, dia_r, dia_c, inv_r, inv_c, vec_r, vec_c, cur_r, cur_c, scl,
    fin, fin_x, fin_r, cell, out_sem,
):
    reg = lax.axis_index("region")
    iz = lax.axis_index("industry")
    core = lax.rem(reg, 2)
    iy = lax.rem(reg // 2, NY)
    ix = reg // (2 * NY)
    kb = core * KO
    ks = KO - kb
    sibling = {"region": reg + 1 - 2 * core}

    def plane(x, y):
        return {"region": (x * NY + y) * 2 + core}

    x_peers = [plane(lax.rem(ix + h, NX), iy) for h in LINE_STEPS]
    y_peers = [plane(ix, lax.rem(iy + h, NY)) for h in LINE_STEPS]
    z_peers = [{"industry": lax.rem(iz + h, NZ)} for h in Z_STEPS]
    p_peers = [
        plane(lax.rem(ix + h, NX), lax.rem(iy + g, NY))
        for h in (2, 1, 3, 0)
        for g in (2, 1, 3, 0)
        if h or g
    ]
    o_peers = [
        {"region": (lax.rem(ix + h, NX) * NY + lax.rem(iy + g, NY)) * 2 + 1 - core}
        for h in (2, 1, 3, 0)
        for g in (2, 1, 3, 0)
    ]
    everyone = z_peers + p_peers + o_peers

    barrier = pltpu.get_barrier_semaphore()
    for peer in everyone:
        pl.semaphore_signal(barrier, inc=1, device_id=peer, device_id_type=MESH)

    def remote(src, dst, ss, rs, peer):
        return pltpu.make_async_remote_copy(
            src_ref=src, dst_ref=dst, send_sem=ss, recv_sem=rs, device_id=peer, device_id_type=MESH
        )

    def in_copies(k):
        return [
            pltpu.make_async_copy(a.at[k], b.at[k], in_sem.at[i, k])
            for i, (a, b) in enumerate(((pos_hbm, pos), (low_hbm, low), (high_hbm, high)))
        ]

    small = [
        pltpu.make_async_copy(a, b, small_sem.at[i])
        for i, (a, b) in enumerate(
            ((drow_hbm, drow), (dcol_hbm, dcol), (upper_hbm, upper), (supp_hbm, supp))
        )
    ]
    for c in small:
        c.start()
    for j in range(K):
        for c in in_copies(lax.rem(ks + j, K)):
            c.start()

    for c in small:
        c.wait()

    column = (
        lax.broadcasted_iota(jnp.int32, (S, IL), 0) * (NZ * IL)
        + iz * IL
        + lax.broadcasted_iota(jnp.int32, (S, IL), 1)
    )
    for k in range(K):
        key[k] = jnp.where(column == att_c[k], att_r[k] - reg * RL, -1)

    @pl.loop(0, K)
    def _(k):
        d = drow[k]
        for r in range(RL):
            drow_b[k, pl.ds(r * S, S), :] = jnp.broadcast_to(d[:, r : r + 1], (S, IL))

    for r in range(RL):
        u = upper[r].astype(F32)
        umat[r] = u
        amat[r] = supp[r].astype(F32)
        hmat[r] = BARRIER / u

    lane = lax.broadcasted_iota(jnp.int32, (S, IL), 1)

    @pl.loop(0, K)
    def _(j):
        k = lax.rem(ks + j, K)
        for c in in_copies(k):
            c.wait()
        zero = jnp.zeros((S, IL), F32)
        dc = dcol[k]
        ky = key[k]

        row_s, row_m, col_s, col_m = zero, zero, zero, zero
        if True:
            for r in range(RL):
                rows = pl.ds(r * S, S)
                p = pos[k, r].astype(F32)
                dl = low[k, r].astype(F32)
                du = high[k, r].astype(F32)
                u = umat[r]
                hit = ky == r
                act = jnp.where(hit, 1.0, amat[r])
                om = 1.0 - p
                q = p * om
                den = dl * om + du * p
                rc = 1.0 / (q * den)
                qr = q * rc
                au = act * u
                high_s, low_s = split_pair(au * q * qr)
                sc = high_s.astype(F32) + low_s.astype(F32)
                g = hmat[r] * (om - p) * (den * rc) + jnp.where(hit, WEIGHT_ATTACK, 0.0) - dc
                m = au * (0.5 - p) + sc * (g - drow_b[k, rows, :])
                scal[k, rows, :] = sc
                grad[k, rows, :] = g
                col_s = col_s + sc
                col_m = col_m + m
                row_s = jnp.where(lane == r, jnp.sum(sc, axis=1, keepdims=True), row_s)
                row_m = jnp.where(lane == r, jnp.sum(m, axis=1, keepdims=True), row_m)
        part[k, 0] = row_s
        part[k, 1] = row_m
        part[k, 2] = col_s
        part[k, 3] = col_m

    pl.semaphore_wait(barrier, len(everyone))

    pair_part = remote(part.at[pl.ds(ks, KO)], part_x, pair_s.at[0], pair_r.at[0], sibling)
    pair_scal = remote(scal.at[pl.ds(ks, KO)], scal_x, pair_s.at[1], pair_r.at[1], sibling)
    pair_part.start()
    pair_scal.start()
    pair_part.wait()

    row_s = [part[kb + q, 0] + pltpu.roll(part_x[q, 0], RL, 1) for q in range(KO)]
    row_m = [part[kb + q, 1] + pltpu.roll(part_x[q, 1], RL, 1) for q in range(KO)]
    for q in range(KO):
        for i in range(2):
            ini_c1[q // 2, pl.ds(((q % 2) * 2 + i) * S, S), :] = part[kb + q, 2 + i] + part_x[q, 2 + i]
    packed = [pack(v[2 * i : 2 * i + 2]) for v in (row_s, row_m) for i in range(2)]
    for n in range(12):
        ini_zs[n % 8, 8 * (n // 8) : 8 * (n // 8) + 8, :] = packed[n // 3][8 * (n % 3) : 8 * (n % 3) + 8]
    for n in range(4, 8):
        ini_zs[n, 8:16, :] = jnp.zeros((8, 128), F32)

    def line_start(src, dst, ss, rs, first_x, half):
        along_x = (half == 0) == first_x
        slot = ix if along_x else iy
        for peer in x_peers if along_x else y_peers:
            remote(src.at[half], dst.at[half, slot], ss.at[half], rs.at[half], peer).start()

    def line_finish(src, dst, ss, rs, first_x, half):
        slot = ix if (half == 0) == first_x else iy
        dst[half, slot] = src[half]
        got = dst.at[half, pl.ds(0, 3)]
        c = remote(got, got, ss.at[half], rs.at[half], x_peers[0])
        c.wait_recv()
        c.wait_send()
        return (dst[half, 0] + dst[half, 1]) + (dst[half, 2] + dst[half, 3])

    def tree(t):
        while len(t) > 1:
            t = [t[i] + t[i + 1] for i in range(0, len(t), 2)]
        return t[0]

    def z_start(src, dst, ss, rs):
        for peer in z_peers:
            remote(src, dst.at[iz], ss, rs, peer).start()

    def z_wait(dst, ss, rs):
        got = dst.at[pl.ds(0, NZ - 1)]
        c = remote(got, got, ss, rs, z_peers[0])
        c.wait_recv()
        c.wait_send()

    def z_finish(src, dst, ss, rs):
        dst[iz] = src[...]
        z_wait(dst, ss, rs)
        return tree([dst[i] for i in range(NZ)])

    for h, peer in zip(Z_STEPS, z_peers):
        remote(
            ini_zs.at[lax.rem(iz + h, NZ)], ini_zr.at[iz], ini_s.at[0], ini_r.at[0], peer
        ).start()
    line_1 = (ini_c1, ini_c1r, ini_s.at[pl.ds(1, 2)], ini_r.at[pl.ds(1, 2)], True)
    line_2 = (ini_c2, ini_c2r, ini_s.at[pl.ds(3, 2)], ini_r.at[pl.ds(3, 2)], False)
    for half in range(2):
        line_start(*line_1, half)

    pair_scal.wait()

    def build(t):
        q, s = t // S, lax.rem(t, S)
        own = scal[kb + q, pl.ds(s, RL, stride=S), :]
        other = scal_x[q, pl.ds(s, RL, stride=S), :]
        both = jnp.concatenate([own, other], axis=0)
        h, l = split_pair(both)
        mat_c[q, s, :, 0:IL] = h
        mat_c[q, s, :, IL : 2 * IL] = l
        turned = jnp.transpose(jnp.concatenate([both, jnp.zeros((32, IL), F32)], axis=0))
        h, l = split_pair(turned)
        mat_r[q, s, :, 0:128] = h
        mat_r[q, s, :, 128:256] = l

    HALF_BUILD = KO * S // 2
    pl.loop(0, HALF_BUILD)(build)

    for half in range(2):
        ini_c2[half] = line_finish(*line_1, half)
        line_start(*line_2, half)
    ini_zr[iz] = ini_zs[iz]
    z_wait(ini_zr, ini_s.at[0], ini_r.at[0])
    ini_as[...] = tree([ini_zr[i] for i in range(NZ)])
    z_start(ini_as, ini_ar, ini_s.at[5], ini_r.at[5])

    pl.loop(HALF_BUILD, KO * S)(build)

    for half in range(2):
        total = line_finish(*line_2, half)
        for i in range(2):
            q = 2 * half + i
            d = total[i * 2 * S : i * 2 * S + S] + SHIFT
            m = total[i * 2 * S + S : i * 2 * S + 2 * S]
            inv = 1.0 / d
            dia_c[q] = d
            inv_c[q] = inv
            hist_c[0, q] = m * inv
            cur_c[q] = m * inv
    ini_ar[iz] = ini_as[...]
    z_wait(ini_ar, ini_s.at[5], ini_r.at[5])
    tiles = [ini_ar[n % 8, 8 * (n // 8) : 8 * (n // 8) + 8, :] for n in range(12)]
    sums = []
    for n in range(4):
        sums += unpack(jnp.concatenate(tiles[3 * n : 3 * n + 3], axis=0))
    used = lane < 2 * RL
    for q in range(KO):
        d = sums[q] + SHIFT
        inv = jnp.where(used, 1.0 / d, 0.0)
        dia_r[q] = d
        inv_r[q] = inv
        hist_r[0, q] = sums[KO + q] * inv
        cur_r[q] = sums[KO + q] * inv

    size_of = lax.rem(lax.broadcasted_iota(jnp.int32, (3 * S, 256), 0), S)

    def couple_half(mat, vec, q, depth):
        left = split_three(vec)[:, 0:depth]
        acc = jnp.zeros((3 * S, 256), F32)
        for s in range(S):
            prod = lax.dot_general(
                left, mat[q, s], (((1,), (0,)), ((), ())), preferred_element_type=F32
            )
            acc = jnp.where(size_of == s, prod, acc)
        acc = acc[0:S] + acc[S : 2 * S] + acc[2 * S : 3 * S]
        return acc[:, 0:128] + acc[:, 128:256]

    sub8 = lax.broadcasted_iota(jnp.int32, (8, 128), 0)
    lane8 = lax.broadcasted_iota(jnp.int32, (8, 128), 1)

    def dot_tile(products):
        tile = jnp.zeros((8, 128), F32)
        for d, per in enumerate(products):
            for q in range(KO):
                t = jnp.sum(jnp.sum(per[q], axis=0, keepdims=True), axis=1, keepdims=True)
                tile = jnp.where((sub8 == q) & (lane8 == d), jnp.broadcast_to(t, (8, 128)), tile)
        return tile

    def p_start(n, tile):
        dps[n] = tile
        for peer in p_peers:
            remote(dps.at[n], dpr.at[n, ix * NY + iy], d_ss.at[n], d_rs.at[n], peer).start()

    def p_finish(n):
        dpr[n, ix * NY + iy] = dps[n]
        got = dpr.at[n, pl.ds(0, NX * NY - 1)]
        c = remote(got, got, d_ss.at[n], d_rs.at[n], p_peers[0])
        c.wait_recv()
        c.wait_send()
        return tree([dpr[n, i] for i in range(NX * NY)])

    def zd_start(n, tile):
        dzs[n] = tile
        z_start(dzs.at[n], dzr.at[n], d_ss.at[3 + n], d_rs.at[3 + n])

    def zd_finish(n):
        return z_finish(dzs.at[n], dzr.at[n], d_ss.at[3 + n], d_rs.at[3 + n])

    def value(n, q, d):
        return scl[n, q : q + 1, d : d + 1]

    def advance(j, hist, vec, cur, half):
        mine = range(2 * half, 2 * half + 2)

        @pl.when((j != 2) & (j != 5))
        def _():
            for q in mine:
                cur[q] = hist[j, q]

        @pl.when(j == 2)
        def _():
            for q in mine:
                z0 = hist[0, q] - hist[1, q] + hist[2, q]
                vec[0, q] = z0
                cur[q] = z0

        @pl.when(j == 5)
        def _():
            for q in mine:
                alpha = value(0, q, 0) / value(0, q, 1)
                z0, w1, w3 = vec[0, q], hist[3, q], hist[5, q]
                z1 = z0 - alpha * (z0 + w3)
                vec[1, q] = z1
                vec[2, q] = hist[0, q] - alpha * (z0 + w1)
                vec[3, q] = alpha * z0
                cur[q] = z1

    def send_dots(j, hist, vec, dia, start):
        @pl.when(j == 3)
        def _():
            rz, cv = [], []
            for q in range(KO):
                z0 = vec[0, q]
                dz = dia[q] * z0
                rz.append(dz * hist[0, q])
                cv.append(dz * (z0 + hist[3, q]))
            start(0, dot_tile([rz, cv]))

        @pl.when(j == 6)
        def _():
            rz, zn, zp = [], [], []
            for q in range(KO):
                z1 = vec[1, q]
                dz = dia[q] * z1
                rz.append(dz * vec[2, q])
                zn.append(dz * (z1 + hist[6, q]))
                zp.append(dz * (vec[0, q] + hist[3, q]))
            start(1, dot_tile([rz, zn, zp]))

    @pl.loop(0, ROUNDS + 1)
    def _(j):
        now = lax.rem(j, 2)
        nxt = 1 - now

        def lines(n):
            at = pl.ds(n * 2, 2)
            return (
                (c1.at[n], c1r.at[n], c_ss.at[0, at], c_rs.at[0, at], True),
                (c2.at[n], c2r.at[n], c_ss.at[1, at], c_rs.at[1, at], False),
            )

        def zed(n, half):
            return zs.at[n, half], zr.at[n, half], z_ss.at[n, half], z_rs.at[n, half]

        @pl.when(j > 0)
        def _():
            first, second = lines(now)
            for half in range(2):
                c2[now, half] = line_finish(*first, half)
                line_start(*second, half)

        @pl.when(j == 5)
        def _():
            scl[0] = zd_finish(0) + p_finish(0)

        for half in range(2):

            @pl.when(j > 0)
            def _():
                for i, t in enumerate(unpack(z_finish(*zed(now, half)))):
                    hist_r[j, 2 * half + i] = t * inv_r[2 * half + i]
                advance(j, hist_r, vec_r, cur_r, half)

            @pl.when(j < ROUNDS)
            def _():
                for i in range(2):
                    q = 2 * half + i
                    c1[nxt, half, i * S : (i + 1) * S, :] = couple_half(mat_c, cur_r[q], q, 96)
                line_start(*lines(nxt)[0], half)

            @pl.when(j > 0)
            def _():
                total = line_finish(*lines(now)[1], half)
                for i in range(2):
                    hist_c[j, 2 * half + i] = total[i * S : (i + 1) * S] * inv_c[2 * half + i]
                advance(j, hist_c, vec_c, cur_c, half)

            @pl.when(j < ROUNDS)
            def _():
                mine = range(2 * half, 2 * half + 2)
                zs[nxt, half] = pack([couple_half(mat_r, cur_c[q], q, 128) for q in mine])
                z_start(*zed(nxt, half))

        send_dots(j, hist_r, vec_r, dia_r, p_start)
        send_dots(j, hist_c, vec_c, dia_c, zd_start)

    scl[1] = zd_finish(1) + p_finish(1)
    steps = []
    for q in range(KO):
        beta = value(1, q, 0) / value(0, q, 0)
        curv = value(1, q, 1) + 2.0 * beta * value(1, q, 2) + beta * beta * value(0, q, 1)
        steps.append((beta, curv, value(1, q, 0) / curv))

    def second_step(hist, vec, cur, dia):
        rz, zp, zz = [], [], []
        for q in range(KO):
            beta, _, alpha = steps[q]
            p1 = vec[1, q] + beta * vec[0, q]
            np1 = p1 + hist[6, q] + beta * hist[3, q]
            z2 = vec[1, q] - alpha * (p1 + hist[8, q] + beta * hist[5, q])
            g2 = vec[2, q] - alpha * np1
            vec[3, q] = vec[3, q] + alpha * p1
            vec[4, q] = p1
            cur[q] = z2
            dz = dia[q] * z2
            rz.append(dz * g2)
            zp.append(dz * np1)
            zz.append(dz * z2)
        return [rz, zp, zz]

    dots_c = second_step(hist_c, vec_c, cur_c, dia_c)
    dots_r = second_step(hist_r, vec_r, cur_r, dia_r)
    cross = [2.0 * couple_half(mat_c, cur_r[q], q, 96) * cur_c[q] for q in range(KO)]
    zd_start(2, dot_tile(dots_c + [cross]))

    for i, (vec, cur) in enumerate(((vec_r, cur_r), (vec_c, cur_c))):
        for q in range(KO):
            for n, x in enumerate((vec[3, q], cur[q], vec[4, q])):
                fin[i, n, q] = pltpu.roll(x, 128 - RL, 1) if i == 0 else x
    swap = remote(fin, fin_x, pair_s.at[2], pair_r.at[2], sibling)
    swap.start()

    tile = dot_tile(dots_r)
    for q in range(KO):
        for d, x in ((11, value(1, q, 0)), (12, steps[q][1])):
            tile = jnp.where((sub8 == q) & (lane8 == d), jnp.broadcast_to(x, (8, 128)), tile)
    tile_c = zd_finish(2)
    tile = tile + jnp.where(lane8 == 3, tile_c, 0.0)
    tile = tile + pltpu.roll(jnp.where(lane8 < 3, tile_c, 0.0), 8, 1)
    dps[2] = tile
    chip = core * NX * NY + ix * NY + iy
    for peer in o_peers + p_peers:
        remote(dps.at[2], dfr.at[chip], d_ss.at[2], d_rs.at[2], peer).start()
    dfr[chip] = tile
    got = dfr.at[pl.ds(0, 2 * NX * NY - 1)]
    c = remote(got, got, d_ss.at[2], d_rs.at[2], sibling)
    c.wait_recv()
    c.wait_send()
    swap.wait()
    for owner in range(2):
        own = owner == 0
        who = core if own else 1 - core
        base = kb if own else ks
        total = tree([dfr[who * NX * NY + i] for i in range(NX * NY)])
        same = dfr[who * NX * NY]
        for q in range(KO):

            def both(d):
                return total[q : q + 1, d : d + 1] + same[q : q + 1, d + 8 : d + 9]

            rz2 = both(0)
            beta = rz2 / same[q : q + 1, 11:12]
            curv = (
                both(2) + total[q : q + 1, 3:4]
                + 2.0 * beta * both(1) + beta * beta * same[q : q + 1, 12:13]
            )
            alpha = rz2 / curv
            if own:
                row = (vec_r[3, q], cur_r[q], vec_r[4, q])
                col = (vec_c[3, q], cur_c[q], vec_c[4, q])
            else:
                row = (fin_x[0, 0, q], fin_x[0, 1, q], fin_x[0, 2, q])
                col = (fin_x[1, 0, q], fin_x[1, 1, q], fin_x[1, 2, q])
            fin_r[base + q] = row[0] + alpha * (row[1] + beta * row[2])
            col_out[base + q] = col[0] + alpha * (col[1] + beta * col[2])

    @pl.loop(0, K)
    def _(k):
        y = fin_r[k]
        row_out[k] = y
        y = y + drow[k]
        c = col_out[k]
        for r in range(RL):
            rows = pl.ds(r * S, S)
            t = jnp.broadcast_to(y[:, r : r + 1], (S, IL)) + (c - grad[k, rows, :])
            cell[k, r] = (scal[k, rows, :] * t).astype(BF16)
        pltpu.make_async_copy(cell.at[k], cell_hbm.at[k], out_sem.at[k]).start()

    for k in range(K):
        pltpu.make_async_copy(cell.at[k], cell_hbm.at[k], out_sem.at[k]).wait()


def local(pos, low, high, upper, supp, att_r, att_c, drow, dcol):
    turned = jnp.pad(jnp.transpose(drow, (0, 2, 1)), ((0, 0), (0, 0), (0, 128 - RL)))
    V, DMA = pltpu.VMEM, pltpu.SemaphoreType.DMA
    cells = (K, RL, S, IL)
    scratch = [
        V(cells, BF16), V(cells, BF16), V(cells, BF16),
        V((RL, S, IL), jnp.int32), V((RL, S, IL), jnp.int32),
        V((K, S, 128), F32), V((K, S, IL), F32),
        DMA((3, K)), DMA((4,)),
        V((K, RL * S, IL), F32), V((KO, RL * S, IL), F32), V((K, RL * S, IL), F32),
        V((K, RL * S, IL), F32),
        V((RL, S, IL), F32), V((RL, S, IL), F32), V((RL, S, IL), F32),
        V((K, S, IL), jnp.int32),
        V((K, 4, S, 128), F32), V((KO, 4, S, 128), F32), DMA((3,)), DMA((3,)),
        V((KO, S, 2 * RL, 2 * IL), BF16), V((KO, S, IL, 256), BF16),
        V((NZ, 16, 128), F32), V((NZ, 16, 128), F32), V((16, 128), F32), V((NZ, 16, 128), F32),
        V((2, 64, 128), F32), V((2, 4, 64, 128), F32), V((2, 64, 128), F32), V((2, 4, 64, 128), F32),
        DMA((6,)), DMA((6,)),
        V((2, 2, 24, 128), F32), V((2, 2, NZ, 24, 128), F32), DMA((2, 2)), DMA((2, 2)),
        V((2, 2, 32, 128), F32), V((2, 2, 4, 32, 128), F32),
        V((2, 2, 32, 128), F32), V((2, 2, 4, 32, 128), F32),
        DMA((2, 4)), DMA((2, 4)),
        V((3, 8, 128), F32), V((3, NZ, 8, 128), F32), V((3, 8, 128), F32), V((3, NX * NY, 8, 128), F32),
        V((2 * NX * NY, 8, 128), F32),
        DMA((6,)), DMA((6,)),
        V((ROUNDS + 1, KO, S, 128), F32), V((ROUNDS + 1, KO, S, 128), F32),
        V((KO, S, 128), F32), V((KO, S, 128), F32), V((KO, S, 128), F32), V((KO, S, 128), F32),
        V((5, KO, S, 128), F32), V((5, KO, S, 128), F32),
        V((KO, S, 128), F32), V((KO, S, 128), F32),
        V((3, 8, 128), F32),
        V((2, 3, KO, S, 128), F32), V((2, 3, KO, S, 128), F32), V((K, S, 128), F32),
        V(cells, BF16), DMA((K,)),
    ]
    any_spec = pl.BlockSpec(memory_space=pl.ANY)
    hbm_spec = pl.BlockSpec(memory_space=pltpu.HBM)
    smem_spec = pl.BlockSpec(memory_space=pltpu.SMEM)
    vmem_spec = pl.BlockSpec(memory_space=pltpu.VMEM)
    cell, row, col = pl.pallas_call(
        kernel,
        out_shape=(
            jax.ShapeDtypeStruct(cells, BF16),
            jax.ShapeDtypeStruct((K, S, 128), F32),
            jax.ShapeDtypeStruct((K, S, IL), F32),
        ),
        in_specs=[hbm_spec] * 5 + [smem_spec] * 2 + [hbm_spec] * 2,
        out_specs=(any_spec, vmem_spec, vmem_spec),
        scratch_shapes=scratch,
        compiler_params=pltpu.CompilerParams(
            collective_id=0, has_side_effects=True, vmem_limit_bytes=VL * 1024 * 1024
        ),
    )(pos, low, high, upper, supp, att_r, att_c, turned, dcol)
    return cell, jnp.transpose(row[:, :, :RL], (0, 2, 1)), col


def solution(mesh):
    cells = P(None, "region", None, "industry")
    return jax.shard_map(
        local,
        mesh=mesh,
        in_specs=(
            cells, cells, cells,
            P("region", None, "industry"), P("region", None, "industry"),
            P(), P(), P(None, "region", None), P(None, None, "industry"),
        ),
        out_specs=(cells, P(None, "region", None), P(None, None, "industry")),
        check_vma=False,
    )
```
